256 devices in a mesh: ns: 64 (over z_lo, y, x), ew: 4 (over z_hi, core).
Axes of the slice: x: 4, y: 4, z: 8 (z_hi: 2, z_lo: 4; z = z_hi * 4 + z_lo), core: 2. Of those that a mesh axis runs over, the one named last changes fastest.
Arguments:
- tokens: bfloat16 [512, 512, 512], P('ns', 'ew'), may hold values from -6 to 6
- conv_gain: float32 [512], replicated, may hold values from 0.1 to 1.9
- w_expand: bfloat16 [512, 2048], replicated, may hold values from -0.25 to 0.25
- dw_kernel: float32 [3, 3, 2048], replicated, may hold values from -2 to 2
- w_project: bfloat16 [2048, 512], replicated, may hold values from -0.375 to 0.375
- block_gain: float32 [512], replicated, may hold values from 0.1 to 1.9
- block_qkv: bfloat16 [512, 1536], replicated, may hold values from -2 to 2
- block_out: bfloat16 [512, 512], replicated, may hold values from -0.25 to 0.25
- grid_gain: float32 [512], replicated, may hold values from 0.1 to 1.9
- grid_qkv: bfloat16 [512, 1536], replicated, may hold values from -2 to 2
- grid_out: bfloat16 [512, 512], replicated, may hold values from -0.25 to 0.25
Outputs:
- block_output: bfloat16 [512, 512, 512], P('ns', 'ew')
The draws below stay inside these ranges and needn't reach their ends.
All inputs are finite; a program needn't handle non-finite values.
Results may differ from the reference program's by a relative error of at most 0.017.
Values may be sent and summed in bfloat16 or wider, within the bound.
A program may use at most 128 MiB of HBM per device.

```python
import math
import jax
import jax.numpy as jnp
from jax import lax

C = 512
HEADS = 16
FFH = 2048
WINDOW = 8
ROWS = 512
COLS = 512


def projection_draw(base_key):
    key_query, key_key, key_value = jax.random.split(base_key, 3)
    queries = jax.random.normal(key_query, (C, C), jnp.float32) * (2.0 / math.sqrt(C))
    key_cols = jax.random.normal(key_key, (C, C), jnp.float32) * (2.0 / math.sqrt(C))
    value_cols = jax.random.normal(key_value, (C, C), jnp.float32) * (1.0 / math.sqrt(C))
    joined = jnp.concatenate([queries, key_cols, value_cols], axis=1)
    return jnp.clip(joined, -2.0, 2.0).astype(jnp.bfloat16)


def draw_block_qkv(key, part):
    return projection_draw(jax.random.fold_in(key, 11))


def draw_grid_qkv(key, part):
    return projection_draw(jax.random.fold_in(key, 23))


def block_levels(own_key, dims, shards, least, largest):
    gain = 1.0
    for axis_at, shards_of in shards:
        draws = jax.random.uniform(jax.random.fold_in(jax.random.fold_in(own_key, 6), axis_at), (shards_of,), jnp.float32, least / len(shards), largest / len(shards))
        gain = gain * jnp.repeat(jnp.exp(draws), dims[axis_at] // shards_of).reshape((-1,) + (1,) * (len(dims) - 1 - axis_at))
    return gain


def centred(rng, extent, scale, reach, shards=(), held_as=jnp.bfloat16):
    entries = scale * jax.random.normal(rng, extent, jnp.float32)
    if shards:
        entries = entries * block_levels(rng, extent, shards, -0.22, 0.18)
    return jnp.clip(entries, -reach, reach).astype(held_as)


def setup_inputs(seed: int = 0) -> dict:
    arg_keys = jax.random.split(jax.random.key(seed), 12)
    tokens = centred(arg_keys[0], (ROWS, COLS, C), 1.0, 6.0, ((0, 64), (1, 4)))
    conv_gain = jnp.clip(1.0 + 0.18 * jax.random.normal(arg_keys[1], (C,), jnp.float32), 0.1, 1.9)
    w_expand = centred(arg_keys[2], (C, FFH), C ** -0.5, 0.25)
    dw_kernel = centred(arg_keys[3], (3, 3, FFH), 9 ** -0.5, 2.0, (), jnp.float32)
    w_project = centred(arg_keys[4], (FFH, C), (FFH // 9) ** -0.5, 0.375)
    block_gain = jnp.clip(1.0 + 0.18 * jax.random.normal(arg_keys[5], (C,), jnp.float32), 0.1, 1.9)
    block_qkv = draw_block_qkv(jax.random.fold_in(arg_keys[11], 71), 0)
    block_out = centred(arg_keys[7], (C, C), C ** -0.5, 0.25)
    grid_gain = jnp.clip(1.0 + 0.18 * jax.random.normal(arg_keys[8], (C,), jnp.float32), 0.1, 1.9)
    grid_qkv = draw_grid_qkv(jax.random.fold_in(arg_keys[11], 71), 0)
    grid_out = centred(arg_keys[10], (C, C), C ** -0.5, 0.25)
    return dict(tokens=tokens, conv_gain=conv_gain, w_expand=w_expand, dw_kernel=dw_kernel, w_project=w_project, block_gain=block_gain, block_qkv=block_qkv, block_out=block_out, grid_gain=grid_gain, grid_qkv=grid_qkv, grid_out=grid_out)


def normalize(tokens, scale_gain):
    floats = tokens.astype(jnp.float32)
    center = floats - lax.optimization_barrier(jnp.mean(floats, axis=-1, keepdims=True))
    spread = lax.optimization_barrier(jnp.mean(center * center, axis=-1, keepdims=True))
    return (center * lax.rsqrt(spread + 1e-05) * scale_gain.astype(jnp.float32)).astype(jnp.bfloat16)

def expand_rows(tokens, scale_gain, w_expand):
    normed = normalize(tokens, scale_gain)
    flat_tokens = normed.reshape(-1, normed.shape[-1])
    hidden = jax.nn.gelu(jnp.dot(flat_tokens, w_expand, preferred_element_type=jnp.float32))
    return hidden.astype(jnp.bfloat16).reshape(tokens.shape[:-1] + (w_expand.shape[1],))

def depthwise(padded, dw_kernel, tile_rows, tile_cols):
    summed = jnp.zeros((tile_rows, tile_cols, padded.shape[-1]), jnp.float32)
    for offset_row in range(3):
        for offset_col in range(3):
            summed = summed + padded[offset_row:offset_row + tile_rows, offset_col:offset_col + tile_cols].astype(jnp.float32) * dw_kernel[offset_row, offset_col]
    return jax.nn.gelu(summed).astype(jnp.bfloat16)

def attend(tokens, scale_gain, w_qkv, w_out):
    layout = tokens.shape
    dim_p, dim_w, dim_q, dim_s, channels = layout
    head_dim = channels // HEADS
    normed = normalize(tokens, scale_gain).reshape(-1, channels)
    packed = jnp.dot(normed, w_qkv, preferred_element_type=jnp.float32).astype(jnp.bfloat16)
    packed = packed.reshape(dim_p, dim_w, dim_q, dim_s, 3, HEADS, head_dim)
    moved = jnp.transpose(packed, (4, 1, 3, 5, 0, 2, 6)).reshape(3, dim_w * dim_s, HEADS, dim_p * dim_q, head_dim)
    queries = moved[0].astype(jnp.float32)
    key_rows = moved[1].astype(jnp.float32)
    value_rows = moved[2].astype(jnp.float32)
    scores = jnp.einsum('nhqd,nhkd->nhqk', queries, key_rows) * head_dim ** (-0.5)
    weights = jax.nn.softmax(scores, axis=-1).astype(jnp.bfloat16)
    blended = jnp.einsum('nhqk,nhkd->nhqd', weights.astype(jnp.float32), value_rows).astype(jnp.bfloat16)
    blended = blended.reshape(dim_w, dim_s, HEADS, dim_p, dim_q, head_dim)
    blended = jnp.transpose(blended, (3, 0, 4, 1, 2, 5)).reshape(-1, channels)
    result = tokens.astype(jnp.float32).reshape(-1, channels) + jnp.dot(blended, w_out, preferred_element_type=jnp.float32)
    return result.astype(jnp.bfloat16).reshape(layout)

def reference(tokens, conv_gain, w_expand, dw_kernel, w_project, block_gain, block_qkv, block_out, grid_gain, grid_qkv, grid_out):
    rows_all, cols_all, channels = tokens.shape
    padded_rows = jnp.pad(tokens, ((1, 1), (0, 0), (0, 0)))

    def conv_band(band_index):
        row_start = band_index * WINDOW
        slab_rows = lax.dynamic_slice_in_dim(padded_rows, row_start, WINDOW + 2, 0)
        hidden = expand_rows(slab_rows, conv_gain, w_expand)
        position = row_start - 1 + jnp.arange(WINDOW + 2, dtype=jnp.int32)
        inside = (position >= 0) & (position < rows_all)
        hidden = jnp.where(inside[:, None, None], hidden, jnp.zeros_like(hidden))
        hidden = jnp.pad(hidden, ((0, 0), (1, 1), (0, 0)))
        active = depthwise(hidden, dw_kernel, WINDOW, cols_all)
        center = lax.dynamic_slice_in_dim(tokens, row_start, WINDOW, 0)
        update = jnp.dot(active.reshape(-1, active.shape[-1]), w_project, preferred_element_type=jnp.float32)
        return (center.astype(jnp.float32) + update.reshape(WINDOW, cols_all, channels)).astype(jnp.bfloat16)
    band_ids = jnp.arange(rows_all // WINDOW, dtype=jnp.int32)
    after_conv = lax.map(conv_band, band_ids).reshape(rows_all, cols_all, channels)

    def block_band(band_tokens):
        shaped = band_tokens.reshape(WINDOW, cols_all // WINDOW, WINDOW, 1, channels)
        return attend(shaped, block_gain, block_qkv, block_out).reshape(WINDOW, cols_all, channels)
    after_block = lax.map(block_band, after_conv.reshape(rows_all // WINDOW, WINDOW, cols_all, channels))
    after_block = after_block.reshape(rows_all, cols_all, channels)
    stride_rows = rows_all // WINDOW
    stride_cols = cols_all // WINDOW
    grouped = jnp.moveaxis(after_block.reshape(WINDOW, stride_rows, WINDOW, stride_cols, channels), 1, 0)

    def grid_row(row_tokens):
        shaped = row_tokens.reshape(WINDOW, 1, WINDOW, stride_cols, channels)
        return attend(shaped, grid_gain, grid_qkv, grid_out).reshape(WINDOW, WINDOW, stride_cols, channels)
    mixed_rows = lax.map(grid_row, grouped)
    return jnp.moveaxis(mixed_rows, 0, 1).reshape(rows_all, cols_all, channels)
```

```python
import functools
import math

import jax
import jax.numpy as jnp
from jax import lax
from jax.experimental import pallas as pl
from jax.experimental.pallas import tpu as pltpu
from jax.sharding import PartitionSpec as P

MESH = pl.DeviceIdType.MESH
BF = jnp.bfloat16
F32 = jnp.float32
HEADS = 16
EXP_SCALE = math.log2(math.e) / math.sqrt(32.0)
GELU_A = math.sqrt(2.0 / math.pi)
GELU_B = GELU_A * 0.044715


def gelu(x):
    half = 0.5 * x
    t = jnp.tanh(x * (GELU_A + GELU_B * (x * x)))
    return half + half * t


def layer_norm(x, gain):
    center = x - jnp.mean(x, axis=-1, keepdims=True)
    spread = jnp.mean(center * center, axis=-1, keepdims=True)
    return (center * lax.rsqrt(spread + 1e-05) * gain).astype(BF)


def dot(a, b):
    return jnp.dot(a, b, preferred_element_type=F32)


def head_mask(head):
    lane = lax.broadcasted_iota(jnp.int32, (1, 128), 1)
    return (lane >= head * 32) & (lane < head * 32 + 32)


def attend_window(qkv, row, heads_out, out_row):
    zero = jnp.zeros((64, 128), BF)
    one = jnp.ones((64, 128), BF)
    low = lax.broadcasted_iota(jnp.int32, (1, 128), 1) < 64
    for group in range(4):
        lanes = 128 * group
        q = qkv[pl.ds(row, 64), lanes : lanes + 128]
        k = qkv[pl.ds(row, 64), 512 + lanes : 512 + lanes + 128]
        v = qkv[pl.ds(row, 64), 1024 + lanes : 1024 + lanes + 128]
        masks = [jnp.broadcast_to(head_mask(h), (64, 128)) for h in range(4)]
        keys = jnp.concatenate([jnp.where(m, k, zero) for m in masks], axis=0)
        values = jnp.concatenate([jnp.where(m, v, zero) for m in masks], axis=0)
        ones = jnp.concatenate([jnp.where(m, one, zero) for m in masks], axis=0)
        scores = lax.dot_general(q, keys, (((1,), (1,)), ((), ())), preferred_element_type=F32)
        parts = []
        for t in range(2):
            s = scores[:, 128 * t : 128 * t + 128]
            top_low = jnp.max(jnp.where(low, s, -jnp.inf), axis=1, keepdims=True)
            top_high = jnp.max(jnp.where(low, -jnp.inf, s), axis=1, keepdims=True)
            top = jnp.where(low, top_low, top_high)
            parts.append(jnp.exp2((s - top) * EXP_SCALE).astype(BF))
        weights = jnp.concatenate(parts, axis=1)
        both = dot(weights, jnp.concatenate([values, ones], axis=1))
        heads_out[pl.ds(out_row, 64), lanes : lanes + 128] = (both[:, :128] / both[:, 128:]).astype(BF)


def kernel(
    tok_hbm, conv_gain, we_hbm, dw, wp_hbm, block_gain, bqkv_hbm, bo_hbm, grid_gain, gqkv_hbm, go_hbm,
    out,
    tok, we, wp, bqkv, bo, gqkv, go,
    halo_n, halo_s, halo_w, halo_e,
    normed, normed_halo, normed_edge, expanded, acc, packed, heads_out, send1, recv1, send2, perm, unperm,
    weight_sem, halo_send, halo_recv, send1_sem, recv1_sem, send2_sem, recv2_sem, local_sem,
):
    n = lax.axis_index("ns")
    e = lax.axis_index("ew")
    a_me = n // 8
    rho = n % 8
    me = a_me * 4 + e
    north, south = (n + 63) % 64, (n + 1) % 64
    west, east = (e + 3) % 4, (e + 1) % 4

    def device(p):
        return (p // 4 * 8 + rho, p % 4)

    barrier = pltpu.get_barrier_semaphore()

    def greet(k, c):
        pl.semaphore_signal(barrier, inc=1, device_id=device((me + k) % 32), device_id_type=MESH)
        return c

    lax.fori_loop(1, 32, greet, 0)
    for row_band in (north, south):
        for strip in (west, e, east):
            pl.semaphore_signal(barrier, inc=1, device_id=(row_band, strip), device_id_type=MESH)

    loads = [
        pltpu.make_async_copy(src, dst, weight_sem.at[i])
        for i, (src, dst) in enumerate(
            [(tok_hbm, tok), (we_hbm, we), (wp_hbm, wp), (bqkv_hbm, bqkv), (bo_hbm, bo), (gqkv_hbm, gqkv), (go_hbm, go)]
        )
    ]
    for load in loads:
        load.start()
    pl.semaphore_wait(barrier, 37)

    moves = [
        (tok_hbm.at[0], halo_s, (north, e)),
        (tok_hbm.at[7], halo_n, (south, e)),
        (tok_hbm.at[:, 0:8], halo_e.at[1:9], (n, west)),
        (tok_hbm.at[:, 120:128], halo_w.at[1:9], (n, east)),
        (tok_hbm.at[0, 0:8], halo_e.at[9], (north, west)),
        (tok_hbm.at[0, 120:128], halo_w.at[9], (north, east)),
        (tok_hbm.at[7, 0:8], halo_e.at[0], (south, west)),
        (tok_hbm.at[7, 120:128], halo_w.at[0], (south, east)),
    ]
    halos = [
        pltpu.make_async_remote_copy(
            src_ref=src, dst_ref=dst, send_sem=halo_send.at[i], recv_sem=halo_recv.at[i], device_id=to, device_id_type=MESH
        )
        for i, (src, dst, to) in enumerate(moves)
    ]
    for halo in halos:
        halo.start()

    loads[0].wait()
    gain = conv_gain[...]
    for i in range(8):
        normed[i * 128 : i * 128 + 128, :] = layer_norm(tok[i].astype(F32), gain)
    loads[1].wait()

    def expand_own(f, c):
        cols = pl.ds(pl.multiple_of(f * 256, 256), 256)
        for pair in range(4):
            hidden = gelu(dot(normed[pair * 256 : pair * 256 + 256, :], we[:, cols]))
            for r in range(2):
                for t in range(2):
                    expanded[2 * f + t, 1 + pair * 2 + r, 8:136, :] = hidden[r * 128 : r * 128 + 128, 128 * t : 128 * t + 128]
        return c

    lax.fori_loop(0, 8, expand_own, 0)

    row = lax.broadcasted_iota(jnp.int32, (256, 256), 0)
    col = lax.broadcasted_iota(jnp.int32, (256, 256), 1)
    perm[...] = jnp.where(col == (row & 31) * 8 + (row >> 5), 1.0, 0.0).astype(BF)
    unperm[...] = jnp.where(col == (row & 7) * 32 + (row >> 3), 1.0, 0.0).astype(BF)

    for halo in halos:
        halo.wait()
    zero_row = jnp.zeros((128, 512), BF)
    normed_halo[0:128, :] = jnp.where(n > 0, layer_norm(halo_n[...].astype(F32), gain), zero_row)
    normed_halo[128:256, :] = jnp.where(n < 63, layer_norm(halo_s[...].astype(F32), gain), zero_row)
    pick = lax.broadcasted_iota(jnp.int32, (16, 80), 1) - 8 * lax.broadcasted_iota(jnp.int32, (16, 80), 0)
    edge_row = lax.broadcasted_iota(jnp.int32, (16, 512), 0)
    rows_in = ((edge_row > 0) | (n > 0)) & ((edge_row < 9) | (n < 63))
    for side, (block, at, there) in enumerate([(halo_w, 7, e > 0), (halo_e, 0, e < 3)]):
        chosen = jnp.where(pick == at, 1.0, 0.0).astype(BF)
        tokens_edge = dot(chosen, block[...].reshape(80, 512))
        ned = layer_norm(tokens_edge, gain).astype(F32)
        normed_edge[side * 16 : side * 16 + 16, :] = jnp.where(rows_in & there, ned, 0.0).astype(BF)

    def expand_halo(f, c):
        cols = pl.ds(pl.multiple_of(f * 256, 256), 256)
        hidden = gelu(dot(normed_halo[...], we[:, cols]))
        edge = gelu(dot(normed_edge[...], we[:, cols]))
        for t in range(2):
            lanes = slice(128 * t, 128 * t + 128)
            expanded[2 * f + t, 0, 8:136, :] = hidden[0:128, lanes]
            expanded[2 * f + t, 9, 8:136, :] = hidden[128:256, lanes]
            for r in range(10):
                expanded[2 * f + t, r, 7:8, :] = edge[r : r + 1, lanes]
                expanded[2 * f + t, r, 136:137, :] = edge[16 + r : 17 + r, lanes]
        return c

    lax.fori_loop(0, 8, expand_halo, 0)
    for load in loads[2:]:
        load.wait()

    for quarter in range(4):

        def conv(f, c, quarter=quarter):
            pieces = []
            for t in range(4):
                lane_tile = 4 * f + t
                lanes = pl.ds(pl.multiple_of(f * 512 + t * 128, 128), 128)
                taps = [[dw[a, b : b + 1, lanes] for b in range(3)] for a in range(3)]
                rows = [[None, None] for _ in range(8)]
                for seg in range(2):
                    start = 64 * seg + 16 * quarter + 7
                    loaded = [
                        [expanded[lane_tile, r, start + b : start + b + 16, :] for b in range(3)] for r in range(10)
                    ]
                    for i in range(8):
                        total = None
                        for a in range(3):
                            for b in range(3):
                                term = loaded[i + a][b] * taps[a][b]
                                total = term if total is None else total + term
                        rows[i][seg] = gelu(total).astype(BF)
                pieces.append(jnp.concatenate([rows[i][s] for i in range(8) for s in range(2)], axis=0))
            active = jnp.concatenate(pieces, axis=1)
            update = dot(active, wp[pl.ds(pl.multiple_of(f * 512, 512), 512), :])

            @pl.when(f == 0)
            def _():
                acc[...] = update

            @pl.when(f > 0)
            def _():
                acc[...] += update

            return c

        lax.fori_loop(0, 4, conv, 0)
        windows = []
        for seg in range(2):
            for j2 in range(2):
                for i in range(8):
                    c0 = 16 * quarter + 8 * j2
                    windows.append(
                        acc[i * 32 + seg * 16 + 8 * j2 : i * 32 + seg * 16 + 8 * j2 + 8, :]
                        + tok[i, 64 * seg + c0 : 64 * seg + c0 + 8, :].astype(F32)
                    )
        x = jnp.concatenate(windows, axis=0).astype(BF).astype(F32)
        acc[...] = x
        packed[0:256, :] = dot(layer_norm(x, block_gain[...]), bqkv[...]).astype(BF)

        def window(w, c):
            at = pl.multiple_of(w * 64, 64)
            attend_window(packed, at, heads_out, at)
            return c

        lax.fori_loop(0, 4, window, 0)
        acc[...] += dot(heads_out[0:256, :], bo[...])
        for j2 in range(2):
            j = 2 * quarter + j2
            ordered = []
            for i in range(8):
                for seg in range(2):
                    r0 = ((seg * 2 + j2) * 8 + i) * 8
                    ordered.append(acc[r0 : r0 + 8, :])
            send1[j] = jnp.concatenate(ordered, axis=0).astype(BF).reshape(8, 2, 8, 512)
            strip = (j % 2) * 2 + (j // 2) % 2
            half = j // 4

            def send(k, c, j=j, strip=strip, half=half):
                i = jnp.bitwise_xor(a_me, k)
                p = i * 4 + strip

                @pl.when(p != me)
                def _():
                    pltpu.make_async_remote_copy(
                        src_ref=send1.at[j, i],
                        dst_ref=recv1.at[half, me],
                        send_sem=send1_sem.at[j, i],
                        recv_sem=recv1_sem.at[half, me],
                        device_id=device(p),
                        device_id_type=MESH,
                    ).start()

                @pl.when(p == me)
                def _():
                    pltpu.make_async_copy(send1.at[j, i], recv1.at[half, me], local_sem.at[half]).start()

                return c

            lax.fori_loop(0, 8, send, 0)

    for half in range(2):

        def arrive(k, c, half=half):
            p = jnp.bitwise_xor(me, k)
            pltpu.make_async_remote_copy(
                src_ref=send1.at[0, 0],
                dst_ref=recv1.at[half, p],
                send_sem=send1_sem.at[0, 0],
                recv_sem=recv1_sem.at[half, p],
                device_id=device(p),
                device_id_type=MESH,
            ).wait_recv()
            return c

        lax.fori_loop(1, 32, arrive, 0)
        pltpu.make_async_copy(send1.at[0, 0], recv1.at[half, me], local_sem.at[half]).wait()
        for u in range(2):
            x = recv1[half, 16 * u : 16 * u + 16].reshape(256, 512)
            ordered = dot(perm[...], layer_norm(x.astype(F32), grid_gain[...])).astype(BF)
            packed_u = dot(ordered, gqkv[...]).astype(BF)
            for s in range(8):
                packed[s * 64 + 32 * u : s * 64 + 32 * u + 32, :] = packed_u[s * 32 : s * 32 + 32, :]

        def grid_window(w, c):
            at = pl.multiple_of(w * 64, 64)
            attend_window(packed, at, heads_out, at)
            return c

        lax.fori_loop(0, 8, grid_window, 0)
        place = 32 * half + 8 * ((e % 2) * 2 + e // 2)
        for u in range(2):
            mixed = jnp.concatenate([heads_out[s * 64 + 32 * u : s * 64 + 32 * u + 32, :] for s in range(8)], axis=0)
            natural = dot(unperm[...], mixed).astype(BF)
            x = recv1[half, 16 * u : 16 * u + 16].reshape(256, 512).astype(F32)
            result = x + dot(natural, go[...])
            send2[half, 16 * u : 16 * u + 16] = result.astype(BF).reshape(16, 2, 8, 512)

            def give_back(k, c, half=half, u=u):
                p = 16 * u + jnp.bitwise_xor(me % 16, k)
                target = out.at[a_me, :, pl.ds(pl.multiple_of(place, 8), 8), :]

                @pl.when(p != me)
                def _():
                    pltpu.make_async_remote_copy(
                        src_ref=send2.at[half, p],
                        dst_ref=target,
                        send_sem=send2_sem.at[half, p],
                        recv_sem=recv2_sem.at[half, me],
                        device_id=device(p),
                        device_id_type=MESH,
                    ).start()

                @pl.when(p == me)
                def _():
                    pltpu.make_async_copy(send2.at[half, p], target, local_sem.at[2 + half]).start()

                return c

            lax.fori_loop(0, 16, give_back, 0)

    def finish(q, c):
        half = q // 32
        p = q % 32
        i = p // 4
        strip = p % 4
        j = 4 * half + (strip % 2) * 2 + strip // 2
        place = 32 * half + 8 * ((strip % 2) * 2 + strip // 2)
        target = out.at[i, :, pl.ds(pl.multiple_of(place, 8), 8), :]

        @pl.when(p != me)
        def _():
            pltpu.make_async_remote_copy(
                src_ref=send1.at[j, i], dst_ref=recv1.at[half, p], send_sem=send1_sem.at[j, i],
                recv_sem=recv1_sem.at[half, p], device_id=device(p), device_id_type=MESH,
            ).wait_send()
            pltpu.make_async_remote_copy(
                src_ref=send2.at[half, p], dst_ref=target, send_sem=send2_sem.at[half, p],
                recv_sem=recv2_sem.at[half, p], device_id=device(p), device_id_type=MESH,
            ).wait()

        @pl.when(p == me)
        def _():
            pltpu.make_async_copy(send2.at[half, p], target, local_sem.at[2 + half]).wait()

        return c

    lax.fori_loop(0, 64, finish, 0)


def on_device(
    tokens, conv_gain, w_expand, dw_kernel, w_project, block_gain, block_qkv, block_out, grid_gain, grid_qkv, grid_out
):
    whole = pl.BlockSpec(memory_space=pltpu.VMEM)
    anywhere = pl.BlockSpec(memory_space=pl.ANY)
    result = pl.pallas_call(
        kernel,
        out_shape=jax.ShapeDtypeStruct((8, 2, 64, 512), BF),
        in_specs=[anywhere, whole, anywhere, whole, anywhere, whole, anywhere, anywhere, whole, anywhere, anywhere],
        out_specs=anywhere,
        scratch_shapes=[
            pltpu.VMEM((8, 128, 512), BF),
            pltpu.VMEM((512, 2048), BF),
            pltpu.VMEM((2048, 512), BF),
            pltpu.VMEM((512, 1536), BF),
            pltpu.VMEM((512, 512), BF),
            pltpu.VMEM((512, 1536), BF),
            pltpu.VMEM((512, 512), BF),
            pltpu.VMEM((128, 512), BF),
            pltpu.VMEM((128, 512), BF),
            pltpu.VMEM((10, 8, 512), BF),
            pltpu.VMEM((10, 8, 512), BF),
            pltpu.VMEM((1024, 512), BF),
            pltpu.VMEM((256, 512), BF),
            pltpu.VMEM((32, 512), BF),
            pltpu.VMEM((16, 10, 144, 128), F32),
            pltpu.VMEM((256, 512), F32),
            pltpu.VMEM((512, 1536), BF),
            pltpu.VMEM((512, 512), BF),
            pltpu.VMEM((8, 8, 2, 8, 512), BF),
            pltpu.VMEM((2, 32, 2, 8, 512), BF),
            pltpu.VMEM((2, 32, 2, 8, 512), BF),
            pltpu.VMEM((256, 256), BF),
            pltpu.VMEM((256, 256), BF),
            pltpu.SemaphoreType.DMA((7,)),
            pltpu.SemaphoreType.DMA((8,)),
            pltpu.SemaphoreType.DMA((8,)),
            pltpu.SemaphoreType.DMA((8, 8)),
            pltpu.SemaphoreType.DMA((2, 32)),
            pltpu.SemaphoreType.DMA((2, 32)),
            pltpu.SemaphoreType.DMA((2, 32)),
            pltpu.SemaphoreType.DMA((4,)),
        ],
        compiler_params=pltpu.CompilerParams(
            collective_id=0, has_side_effects=True, vmem_limit_bytes=60 * 1024 * 1024
        ),
        name="maxvit",
    )(
        tokens, conv_gain.reshape(1, 512), w_expand, dw_kernel, w_project, block_gain.reshape(1, 512), block_qkv, block_out,
        grid_gain.reshape(1, 512), grid_qkv, grid_out,
    )
    return result.reshape(tokens.shape)


def solution(mesh):
    in_specs = (P("ns", "ew", None), P(), P(), P(), P(), P(), P(), P(), P(), P(), P())
    out_specs = P("ns", "ew", None)
    return jax.shard_map(
        on_device, mesh=mesh, in_specs=in_specs, out_specs=out_specs, check_vma=False
    )
```

```python
import functools
import math

import jax
import jax.numpy as jnp
from jax import lax
from jax.experimental import pallas as pl
from jax.experimental.pallas import tpu as pltpu
from jax.sharding import PartitionSpec as P

MESH = pl.DeviceIdType.MESH
BF = jnp.bfloat16
F32 = jnp.float32
HEADS = 16
EXP_SCALE = math.log2(math.e) / math.sqrt(32.0)
GELU_A = math.sqrt(2.0 / math.pi)
GELU_B = GELU_A * 0.044715


def gelu(x):
    half = 0.5 * x
    t = jnp.tanh(x * (GELU_A + GELU_B * (x * x)))
    return half + half * t


def layer_norm(x, gain):
    center = x - jnp.mean(x, axis=-1, keepdims=True)
    spread = jnp.mean(center * center, axis=-1, keepdims=True)
    return (center * lax.rsqrt(spread + 1e-05) * gain).astype(BF)


def dot(a, b):
    return jnp.dot(a, b, preferred_element_type=F32)


def head_mask(head):
    lane = lax.broadcasted_iota(jnp.int32, (1, 128), 1)
    return (lane >= head * 32) & (lane < head * 32 + 32)


def attend_windows(qkv, rows, heads_out):
    zero = jnp.zeros((64, 128), BF)
    one = jnp.ones((64, 128), BF)
    low = lax.broadcasted_iota(jnp.int32, (1, 128), 1) < 64
    masks = [jnp.broadcast_to(head_mask(h), (64, 128)) for h in range(4)]
    ones = jnp.concatenate([jnp.where(m, one, zero) for m in masks], axis=0)
    jobs = [(row, 128 * group) for row in rows for group in range(4)]
    scores = []
    for row, lanes in jobs:
        q = qkv[pl.ds(row, 64), lanes : lanes + 128]
        k = qkv[pl.ds(row, 64), 512 + lanes : 512 + lanes + 128]
        keys = jnp.concatenate([jnp.where(m, k, zero) for m in masks], axis=0)
        scores.append(lax.dot_general(q, keys, (((1,), (1,)), ((), ())), preferred_element_type=F32))
    weights = []
    for score in scores:
        parts = []
        for t in range(2):
            s = score[:, 128 * t : 128 * t + 128]
            top_low = jnp.max(jnp.where(low, s, -jnp.inf), axis=1, keepdims=True)
            top_high = jnp.max(jnp.where(low, -jnp.inf, s), axis=1, keepdims=True)
            top = jnp.where(low, top_low, top_high)
            parts.append(jnp.exp2((s - top) * EXP_SCALE).astype(BF))
        weights.append(jnp.concatenate(parts, axis=1))
    for (row, lanes), weight in zip(jobs, weights):
        v = qkv[pl.ds(row, 64), 1024 + lanes : 1024 + lanes + 128]
        values = jnp.concatenate([jnp.where(m, v, zero) for m in masks], axis=0)
        both = dot(weight, jnp.concatenate([values, ones], axis=1))
        heads_out[pl.ds(row, 64), lanes : lanes + 128] = (both[:, :128] / both[:, 128:]).astype(BF)


def kernel(
    tok_hbm, conv_gain, we_hbm, dw, wp_hbm, block_gain, bqkv_hbm, bo_hbm, grid_gain, gqkv_hbm, go_hbm,
    out,
    tok, we, wp, bqkv, bo, gqkv, go,
    halo_n, halo_s, halo_w, halo_e,
    lhs, expanded, acc, packed, heads_out, send1, recv1, send2, perm, unperm,
    weight_sem, halo_send, halo_recv, send1_sem, recv1_sem, send2_sem, recv2_sem,
):
    n = lax.axis_index("ns")
    e = lax.axis_index("ew")
    a_me = n // 8
    rho = n % 8
    me = a_me * 4 + e
    north, south = (n + 63) % 64, (n + 1) % 64
    west, east = (e + 3) % 4, (e + 1) % 4

    def device(p):
        return (p // 4 * 8 + rho, p % 4)

    barrier = pltpu.get_barrier_semaphore()

    def greet(k, c):
        pl.semaphore_signal(barrier, inc=1, device_id=device((me + k) % 32), device_id_type=MESH)
        return c

    lax.fori_loop(1, 32, greet, 0)
    for row_band in (north, south):
        for strip in (west, e, east):
            pl.semaphore_signal(barrier, inc=1, device_id=(row_band, strip), device_id_type=MESH)

    loads = [
        pltpu.make_async_copy(src, dst, weight_sem.at[i])
        for i, (src, dst) in enumerate(
            [(tok_hbm, tok), (we_hbm, we), (wp_hbm, wp), (bqkv_hbm, bqkv), (bo_hbm, bo), (gqkv_hbm, gqkv), (go_hbm, go)]
        )
    ]
    loads[0].start()
    loads[1].start()
    pl.semaphore_wait(barrier, 37)

    moves = [
        (tok_hbm.at[0], halo_s, (north, e)),
        (tok_hbm.at[7], halo_n, (south, e)),
        (tok_hbm.at[:, 0:8], halo_e.at[1:9], (n, west)),
        (tok_hbm.at[:, 120:128], halo_w.at[1:9], (n, east)),
        (tok_hbm.at[0, 0:8], halo_e.at[9], (north, west)),
        (tok_hbm.at[0, 120:128], halo_w.at[9], (north, east)),
        (tok_hbm.at[7, 0:8], halo_e.at[0], (south, west)),
        (tok_hbm.at[7, 120:128], halo_w.at[0], (south, east)),
    ]
    halos = [
        pltpu.make_async_remote_copy(
            src_ref=src, dst_ref=dst, send_sem=halo_send.at[i], recv_sem=halo_recv.at[i], device_id=to, device_id_type=MESH
        )
        for i, (src, dst, to) in enumerate(moves)
    ]
    for halo in halos:
        halo.start()

    gain = conv_gain[...]

    def expand(count, places):
        def step(f, c):
            cols = pl.ds(pl.multiple_of(f * 256, 256), 256)
            hidden = gelu(dot(lhs[0:count, :], we[:, cols]))
            at = 0
            for r, c0, width in places:
                for t in range(2 if r is not None else 0):
                    expanded[2 * f + t, r, 8 + c0 : 8 + c0 + width, :] = hidden[at : at + width, 128 * t : 128 * t + 128]
                at += width
            return c

        lax.fori_loop(0, 8, step, 0)

    def stage(at, values):
        lhs[at : at + values.shape[0], :] = values

    def halo_rows(spans):
        above = jnp.concatenate([halo_n[c0 : c0 + width, :].astype(F32) for c0, width in spans], axis=0)
        below = jnp.concatenate([halo_s[c0 : c0 + width, :].astype(F32) for c0, width in spans], axis=0)
        zero = jnp.zeros(above.shape, BF)
        return jnp.concatenate(
            [jnp.where(n > 0, layer_norm(above, gain), zero), jnp.where(n < 63, layer_norm(below, gain), zero)], axis=0
        )

    def own_rows(spans, rows):
        x = jnp.concatenate([tok[i, c0 : c0 + width, :].astype(F32) for i in rows for c0, width in spans], axis=0)
        return layer_norm(x, gain)

    new_spans = [[(0, 24), (56, 32)], [(24, 16), (88, 16)], [(40, 16), (104, 16)], [(120, 8)]]

    loads[0].wait()
    spans = new_spans[0]
    wide = sum(width for _, width in spans)
    for i in range(0, 8, 2):
        stage(i * wide, own_rows(spans, (i, i + 1)))
    loads[1].wait()
    for load in loads[2:]:
        load.start()
    expand(8 * wide, [(1 + i, c0, width) for i in range(8) for c0, width in spans])

    row = lax.broadcasted_iota(jnp.int32, (256, 256), 0)
    col = lax.broadcasted_iota(jnp.int32, (256, 256), 1)
    perm[...] = jnp.where(col == (row & 31) * 8 + (row >> 5), 1.0, 0.0).astype(BF)
    unperm[...] = jnp.where(col == (row & 7) * 32 + (row >> 3), 1.0, 0.0).astype(BF)

    for halo in halos:
        halo.wait()
    stage(0, halo_rows(spans))
    pick = lax.broadcasted_iota(jnp.int32, (16, 80), 1) - 8 * lax.broadcasted_iota(jnp.int32, (16, 80), 0)
    edge_row = lax.broadcasted_iota(jnp.int32, (16, 512), 0)
    rows_in = ((edge_row > 0) | (n > 0)) & ((edge_row < 9) | (n < 63))
    for side, (block, at, there) in enumerate([(halo_w, 7, e > 0), (halo_e, 0, e < 3)]):
        chosen = jnp.where(pick == at, 1.0, 0.0).astype(BF)
        tokens_edge = dot(chosen, block[...].reshape(80, 512))
        ned = layer_norm(tokens_edge, gain).astype(F32)
        stage(2 * wide + side * 16, jnp.where(rows_in & there, ned, 0.0).astype(BF))
    expand(
        2 * wide + 32,
        [(r, c0, width) for r in (0, 9) for c0, width in spans]
        + [(r, -1, 1) for r in range(10)]
        + [(None, None, 6)]
        + [(r, 128, 1) for r in range(10)],
    )
    for load in loads[2:]:
        load.wait()

    for quarter in range(4):
        if quarter:
            spans = new_spans[quarter]
            wide = sum(width for _, width in spans)
            for i in range(0, 8, 2):
                stage(i * wide, own_rows(spans, (i, i + 1)))
            stage(8 * wide, halo_rows(spans))
            expand(10 * wide, [(r, c0, width) for r in (1, 2, 3, 4, 5, 6, 7, 8, 0, 9) for c0, width in spans])

        def conv(f, c, quarter=quarter):
            pieces = []
            for t in range(4):
                lane_tile = 4 * f + t
                lanes = pl.ds(pl.multiple_of(f * 512 + t * 128, 128), 128)
                taps = [[dw[a, b : b + 1, lanes] for b in range(3)] for a in range(3)]
                rows = [[None, None] for _ in range(8)]
                for seg in range(2):
                    start = 64 * seg + 16 * quarter + 7
                    loaded = [
                        [expanded[lane_tile, r, start + b : start + b + 16, :] for b in range(3)] for r in range(10)
                    ]
                    for i in range(8):
                        total = None
                        for a in range(3):
                            for b in range(3):
                                term = loaded[i + a][b] * taps[a][b]
                                total = term if total is None else total + term
                        rows[i][seg] = gelu(total).astype(BF)
                pieces.append(jnp.concatenate([rows[i][s] for i in range(8) for s in range(2)], axis=0))
            active = jnp.concatenate(pieces, axis=1)
            update = dot(active, wp[pl.ds(pl.multiple_of(f * 512, 512), 512), :])

            @pl.when(f == 0)
            def _():
                acc[...] = update

            @pl.when(f > 0)
            def _():
                acc[...] += update

            return c

        lax.fori_loop(0, 4, conv, 0)
        windows = []
        for seg in range(2):
            for j2 in range(2):
                for i in range(8):
                    c0 = 16 * quarter + 8 * j2
                    windows.append(
                        acc[i * 32 + seg * 16 + 8 * j2 : i * 32 + seg * 16 + 8 * j2 + 8, :]
                        + tok[i, 64 * seg + c0 : 64 * seg + c0 + 8, :].astype(F32)
                    )
        x = jnp.concatenate(windows, axis=0).astype(BF).astype(F32)
        acc[...] = x
        packed[0:256, :] = dot(layer_norm(x, block_gain[...]), bqkv[...]).astype(BF)

        def window(w, c):
            attend_windows(packed, [pl.multiple_of(w * 256 + 64 * r, 64) for r in range(4)], heads_out)
            return c

        lax.fori_loop(0, 1, window, 0)
        acc[...] += dot(heads_out[0:256, :], bo[...])
        for j2 in range(2):
            j = 2 * quarter + j2
            ordered = []
            for i in range(8):
                for seg in range(2):
                    r0 = ((seg * 2 + j2) * 8 + i) * 8
                    ordered.append(acc[r0 : r0 + 8, :])
            send1[j] = jnp.concatenate(ordered, axis=0).astype(BF).reshape(8, 2, 8, 512)
            strip = (j % 2) * 2 + (j // 2) % 2
            half = j // 4

            def send(k, c, j=j, strip=strip, half=half):
                i = jnp.bitwise_xor(a_me, k)
                p = i * 4 + strip

                @pl.when(p != me)
                def _():
                    pltpu.make_async_remote_copy(
                        src_ref=send1.at[j, i],
                        dst_ref=recv1.at[half, me],
                        send_sem=send1_sem.at[half],
                        recv_sem=recv1_sem.at[half],
                        device_id=device(p),
                        device_id_type=MESH,
                    ).start()

                @pl.when(p == me)
                def _():
                    pltpu.make_async_copy(send1.at[j, i], recv1.at[half, me], recv1_sem.at[half]).start()

                return c

            lax.fori_loop(0, 8, send, 0)

    for half in range(2):

        pltpu.make_async_copy(recv1.at[half], recv1.at[half], recv1_sem.at[half]).wait()
        for u in range(2):
            x = recv1[half, 16 * u : 16 * u + 16].reshape(256, 512)
            ordered = dot(perm[...], layer_norm(x.astype(F32), grid_gain[...])).astype(BF)
            packed_u = dot(ordered, gqkv[...]).astype(BF)
            for s in range(8):
                packed[s * 64 + 32 * u : s * 64 + 32 * u + 32, :] = packed_u[s * 32 : s * 32 + 32, :]

        def grid_window(w, c):
            attend_windows(packed, [pl.multiple_of(w * 256 + 64 * r, 64) for r in range(4)], heads_out)
            return c

        lax.fori_loop(0, 2, grid_window, 0)
        place = 32 * half + 8 * ((e % 2) * 2 + e // 2)
        for u in range(2):
            mixed = jnp.concatenate([heads_out[s * 64 + 32 * u : s * 64 + 32 * u + 32, :] for s in range(8)], axis=0)
            natural = dot(unperm[...], mixed).astype(BF)
            x = recv1[half, 16 * u : 16 * u + 16].reshape(256, 512).astype(F32)
            result = x + dot(natural, go[...])
            send2[half, 16 * u : 16 * u + 16] = result.astype(BF).reshape(16, 2, 8, 512)

            def give_back(k, c, half=half, u=u):
                p = 16 * u + jnp.bitwise_xor(me % 16, k)
                target = out.at[a_me, :, pl.ds(pl.multiple_of(place, 8), 8), :]

                @pl.when(p != me)
                def _():
                    pltpu.make_async_remote_copy(
                        src_ref=send2.at[half, p],
                        dst_ref=target,
                        send_sem=send2_sem.at[half],
                        recv_sem=recv2_sem,
                        device_id=device(p),
                        device_id_type=MESH,
                    ).start()

                @pl.when(p == me)
                def _():
                    pltpu.make_async_copy(send2.at[half, p], target, recv2_sem).start()

                return c

            lax.fori_loop(0, 16, give_back, 0)

    for half in range(2):
        for sem in (send1_sem, send2_sem):
            sent = send2.at[half, 0:31]
            pltpu.make_async_copy(sent, sent, sem.at[half]).wait()
    pltpu.make_async_copy(out, out, recv2_sem).wait()


def on_device(
    tokens, conv_gain, w_expand, dw_kernel, w_project, block_gain, block_qkv, block_out, grid_gain, grid_qkv, grid_out
):
    whole = pl.BlockSpec(memory_space=pltpu.VMEM)
    anywhere = pl.BlockSpec(memory_space=pl.ANY)
    result = pl.pallas_call(
        kernel,
        out_shape=jax.ShapeDtypeStruct((8, 2, 64, 512), BF),
        in_specs=[anywhere, whole, anywhere, whole, anywhere, whole, anywhere, anywhere, whole, anywhere, anywhere],
        out_specs=anywhere,
        scratch_shapes=[
            pltpu.VMEM((8, 128, 512), BF),
            pltpu.VMEM((512, 2048), BF),
            pltpu.VMEM((2048, 512), BF),
            pltpu.VMEM((512, 1536), BF),
            pltpu.VMEM((512, 512), BF),
            pltpu.VMEM((512, 1536), BF),
            pltpu.VMEM((512, 512), BF),
            pltpu.VMEM((128, 512), BF),
            pltpu.VMEM((128, 512), BF),
            pltpu.VMEM((10, 8, 512), BF),
            pltpu.VMEM((10, 8, 512), BF),
            pltpu.VMEM((448, 512), BF),
            pltpu.VMEM((16, 10, 144, 128), F32),
            pltpu.VMEM((256, 512), F32),
            pltpu.VMEM((512, 1536), BF),
            pltpu.VMEM((512, 512), BF),
            pltpu.VMEM((8, 8, 2, 8, 512), BF),
            pltpu.VMEM((2, 32, 2, 8, 512), BF),
            pltpu.VMEM((2, 32, 2, 8, 512), BF),
            pltpu.VMEM((256, 256), BF),
            pltpu.VMEM((256, 256), BF),
            pltpu.SemaphoreType.DMA((7,)),
            pltpu.SemaphoreType.DMA((8,)),
            pltpu.SemaphoreType.DMA((8,)),
            pltpu.SemaphoreType.DMA((2,)),
            pltpu.SemaphoreType.DMA((2,)),
            pltpu.SemaphoreType.DMA((2,)),
            pltpu.SemaphoreType.DMA,
        ],
        compiler_params=pltpu.CompilerParams(
            collective_id=0, has_side_effects=True, vmem_limit_bytes=60 * 1024 * 1024
        ),
        name="maxvit",
    )(
        tokens, conv_gain.reshape(1, 512), w_expand, dw_kernel, w_project, block_gain.reshape(1, 512), block_qkv, block_out,
        grid_gain.reshape(1, 512), grid_qkv, grid_out,
    )
    return result.reshape(tokens.shape)


def solution(mesh):
    in_specs = (P("ns", "ew", None), P(), P(), P(), P(), P(), P(), P(), P(), P(), P())
    out_specs = P("ns", "ew", None)
    return jax.shard_map(
        on_device, mesh=mesh, in_specs=in_specs, out_specs=out_specs, check_vma=False
    )
```
